32 devices in a mesh: kern: 8 (over y, x, core), fac: 2 (over z_hi), pair: 2 (over z_lo).
Axes of the slice: x: 2, y: 2, z: 4 (z_hi: 2, z_lo: 2; z = z_hi * 2 + z_lo), core: 2. Of those that a mesh axis runs over, the one named last changes fastest.
Arguments:
- points: bfloat16 [32768, 3072], P('kern', ('fac', 'pair')), may hold values from -6 to 6
- factor: float32 [32768, 3072], P(('kern', 'fac', 'pair')), may hold values from -0.02690478 to 0.02690478
- panel_block: int32 [1], replicated, may hold values from 0 to 63
- finished: int32 [1], replicated, may hold values from 1536 to 3072
Outputs:
- panel_factor: float32 [32768, 512], P(('kern', 'fac', 'pair'))
The draws below stay inside these ranges and needn't reach their ends.
Inputs may be any that keep to these rules, and one draw needn't show every extreme that they name: The panel's points are rows 512 * panel_block to 512 * panel_block + 511. Columns of factor from finished on are not used.
All inputs are finite; a program needn't handle non-finite values.
Results may differ from the reference program's by a relative error of at most 0.0006.
Values may be sent and summed in bfloat16 or wider, within the bound.
No kernel may reach another device: no remote copies, remote signals or barrier semaphores. Data moves between devices by JAX's collectives and lax.ppermute only.
A program may use at most 128 MiB of HBM per device.

```python
import jax
import jax.numpy as jnp
from jax import lax

DIN = 3072
FIN = 3072
M_DEV = 1024
P_SIZE = 512
LAYERS = 5
M = 32768


def level_of(own_key, dims, cuts, smallest, high):
    loudness = 1.0
    for dim, blocks in cuts:
        heights = jax.random.uniform(jax.random.fold_in(jax.random.fold_in(own_key, 6), dim), (blocks,), jnp.float32, smallest / len(cuts), high / len(cuts))
        loudness = loudness * jnp.repeat(jnp.exp(heights), dims[dim] // blocks).reshape((-1,) + (1,) * (len(dims) - 1 - dim))
    return loudness


def normal_values(stream_key, extent, width, most, shards=(), kind=jnp.bfloat16):
    factor_of = level_of(stream_key, extent, shards, -0.22, 0.18) if shards else 1.0
    entries = jax.random.normal(stream_key, extent, jnp.float32) * width * factor_of
    return jnp.minimum(jnp.maximum(entries, -most), most).astype(kind)


def setup_inputs(seed: int = 0) -> dict:
    arg_keys = jax.random.split(jax.random.key(seed), 5)
    points = normal_values(arg_keys[0], (M, DIN), 1.0, 6.0, ((0, 8), (1, 4)))
    factor = jnp.clip(jax.random.uniform(arg_keys[1], (M, FIN), jnp.float32, -0.02690478, 0.02690478) * level_of(arg_keys[1], (M, FIN), ((0, 32),), -0.4, 0.0), -0.02690478, 0.02690478)
    panel_block = jax.random.randint(arg_keys[2], (1,), 0, M // P_SIZE).astype(jnp.int32)
    finished = jax.random.randint(arg_keys[3], (1,), FIN // 2, FIN + 1).astype(jnp.int32)
    return dict(points=points, factor=factor, panel_block=panel_block, finished=finished)


RIDGE = 3.0
EPS = 1e-06

def tangent_kernel(products, left_norm, right_norm):
    scales = jnp.sqrt(left_norm * right_norm)
    covariance = products
    tangent = products
    for repeat in range(LAYERS):
        cosine = jnp.clip(covariance / scales, -1.0, 1.0)
        angles = jnp.arccos(cosine)
        covariance = scales * (jnp.sin(angles) + (jnp.pi - angles) * cosine) / jnp.pi
        slopes = (jnp.pi - angles) / jnp.pi
        tangent = covariance + slopes * tangent
    return tangent

def reference(points, factor, panel_block, finished):
    panel_start = (panel_block[0] * P_SIZE).astype(jnp.int32)
    used_count = finished[0]
    panel_points = lax.dynamic_slice_in_dim(points, panel_start, P_SIZE, 0)
    panel_norm = lax.optimization_barrier(jnp.sum(jnp.square(panel_points.astype(jnp.float32)), axis=1)) / DIN + EPS
    column_keep = (jnp.arange(FIN, dtype=jnp.int32) < used_count).astype(jnp.float32)
    panel_rows = lax.dynamic_slice_in_dim(factor, panel_start, P_SIZE, 0) * column_keep[None, :]
    col_index = jnp.arange(P_SIZE, dtype=jnp.int32)

    def one_block(block_index):
        first_row = (block_index * M_DEV).astype(jnp.int32)
        row_points = lax.dynamic_slice_in_dim(points, first_row, M_DEV, 0)
        row_factor = lax.dynamic_slice_in_dim(factor, first_row, M_DEV, 0)
        products = jnp.dot(row_points.astype(jnp.float32), panel_points.T.astype(jnp.float32), preferred_element_type=jnp.float32) / DIN
        row_norm = lax.optimization_barrier(jnp.sum(jnp.square(row_points.astype(jnp.float32)), axis=1)) / DIN + EPS
        kernel = tangent_kernel(products, row_norm[:, None], panel_norm[None, :])
        row_index = first_row + jnp.arange(M_DEV, dtype=jnp.int32)
        kernel = jnp.where(row_index[:, None] == panel_start + col_index[None, :], kernel + RIDGE, kernel)
        return kernel - jnp.dot(row_factor.astype(jnp.float32), panel_rows.T.astype(jnp.float32), precision=lax.Precision.HIGHEST, preferred_element_type=jnp.float32)
    updated = lax.map(one_block, jnp.arange(M // M_DEV, dtype=jnp.int32)).reshape(M, P_SIZE)
    diag_block = lax.dynamic_slice_in_dim(updated, panel_start, P_SIZE, 0)
    lower_factor = jnp.linalg.cholesky(diag_block)
    return lax.linalg.triangular_solve(lower_factor, updated, left_side=False, lower=True, transpose_a=True)
```

```python
import functools

import jax
import jax.numpy as jnp
from jax import lax
from jax.experimental import pallas as pl
from jax.experimental.pallas import tpu as pltpu
from jax.sharding import PartitionSpec as P

DIN = 3072
P_SIZE = 512
LAYERS = 5
RIDGE = 3.0
EPS = 1e-06
CODES = 32760.0
TINY = 1e-30
BLOCK = 128
ACOS = (
    1.5707963050,
    -0.2145988016,
    0.0889789874,
    -0.0501743046,
    0.0308918810,
    -0.0170881256,
    0.0066700901,
    -0.0012624911,
)


def exchange(value, axis, bit):
    size = lax.axis_size(axis)
    return lax.ppermute(value, axis, [(i, i ^ (1 << bit)) for i in range(size)])


def bit_of(index, bit):
    return lax.bitwise_and(lax.shift_right_logical(index, bit), 1)


def halve(value, axis, bit, root):
    mine = bit_of(lax.axis_index(axis), bit)
    rows = value.shape[0] // 2
    low, high = value[:rows], value[rows:]
    got = exchange(jnp.where(mine == 0, high, low), axis, bit)
    return jnp.where(mine == bit_of(root, bit), jnp.where(mine == 0, low, high), got)


def join(value, axis, bit):
    mine = bit_of(lax.axis_index(axis), bit)
    got = exchange(value, axis, bit)
    return jnp.concatenate(
        [jnp.where(mine == 0, value, got), jnp.where(mine == 0, got, value)], axis=0
    )


def spread(value, axis, bit, root):
    mine = bit_of(lax.axis_index(axis), bit)
    got = exchange(value, axis, bit)
    return jnp.where(mine == bit_of(root, bit), value, got)


def bits_of(axis):
    return list(range((lax.axis_size(axis) - 1).bit_length()))


def root_of(value):
    return value * lax.rsqrt(jnp.maximum(value, TINY))


def arc_part(cosine):
    gap = jnp.maximum(1.0 - cosine, 0.0)
    poly = jnp.full_like(cosine, ACOS[-1] / jnp.pi)
    for term in ACOS[-2::-1]:
        poly = poly * cosine + term / jnp.pi
    return root_of(gap) * poly, root_of(gap * (1.0 + cosine)) * (1.0 / jnp.pi)


def tangent_ratio(cosine):
    cosine = jnp.clip(cosine, -1.0, 1.0)
    angle, sine = arc_part(jnp.abs(cosine))
    slope = jnp.where(cosine < 0.0, angle, 1.0 - angle)
    tangent = cosine
    cosine = slope * cosine + sine
    tangent = slope * tangent + cosine
    for _ in range(LAYERS - 1):
        cosine = jnp.minimum(cosine, 1.0)
        angle, sine = arc_part(cosine)
        slope = 1.0 - angle
        cosine = slope * cosine + sine
        tangent = slope * tangent + cosine
    return tangent


def eliminate(block, unit):
    size = block.shape[0]
    groups = size // 8
    left = [block[8 * g : 8 * g + 8] for g in range(groups)]
    right = [unit[8 * g : 8 * g + 8] for g in range(groups)]
    shape = (8, size)
    sub = lax.broadcasted_iota(jnp.int32, shape, 0)
    scaled = []
    for g in range(groups):
        columns = [
            jnp.broadcast_to(left[g][:, 8 * g + k : 8 * g + k + 1], shape) for k in range(8)
        ]
        steps, left_rows, right_rows = {}, [], []
        pivots = None
        for k in range(8):
            inverse = 1.0 / jnp.broadcast_to(columns[k][k : k + 1], shape)
            pivots = inverse if pivots is None else jnp.where(sub == k, inverse, pivots)
            below = jnp.where(sub > k, columns[k], 0.0)
            left_rows.append(jnp.broadcast_to(left[g][k : k + 1], shape) * inverse)
            right_rows.append(jnp.broadcast_to(right[g][k : k + 1], shape) * inverse)
            for m in range(k + 1, 8):
                steps[k, m] = jnp.broadcast_to(columns[m][k : k + 1], shape) * inverse
                columns[m] = columns[m] - below * steps[k, m]
            if k < 7:
                left[g] = left[g] - below * left_rows[k]
                right[g] = right[g] - below * right_rows[k]
        scaled.append(right[g] * jnp.sqrt(pivots))
        for h in range(g + 1, groups):
            columns = [
                jnp.broadcast_to(left[h][:, 8 * g + k : 8 * g + k + 1], shape) for k in range(8)
            ]
            for k in range(8):
                for m in range(k + 1, 8):
                    columns[m] = columns[m] - columns[k] * steps[k, m]
                left[h] = left[h] - columns[k] * left_rows[k]
                right[h] = right[h] - columns[k] * right_rows[k]
    return jnp.concatenate(scaled, 0)


def exact_dot(a, b, dims):
    return lax.dot_general(
        a, b, (dims, ((), ())), preferred_element_type=jnp.float32, precision=lax.Precision.HIGHEST
    )


def factor_kernel(kernel_ref, rows_ref, high_ref, low_ref, work):
    size = kernel_ref.shape[0]
    blocks = size // BLOCK
    work[:, :size] = kernel_ref[...] - lax.dot_general(
        rows_ref[...],
        rows_ref[...],
        (((1,), (1,)), ((), ())),
        preferred_element_type=jnp.float32,
    )
    shape = (size, size)
    work[:, size:] = jnp.where(
        lax.broadcasted_iota(jnp.int32, shape, 0) == lax.broadcasted_iota(jnp.int32, shape, 1),
        1.0,
        0.0,
    )
    for k in range(blocks):
        lo, hi = k * BLOCK, (k + 1) * BLOCK
        small = eliminate(work[lo:hi, lo:hi], work[lo:hi, size + lo : size + hi])
        wide = small
        if k > 0:
            wide = jnp.concatenate(
                [exact_dot(small, work[lo:hi, size : size + lo], ((1,), (0,))), small], 1
            )
        if k + 1 < blocks:
            upper = exact_dot(small, work[lo:hi, hi:size], ((1,), (0,)))
            rest = exact_dot(upper, jnp.concatenate([upper, wide], 1), ((0,), (0,)))
            work[hi:size, hi : size + hi] = work[hi:size, hi : size + hi] - rest
            wide = jnp.concatenate([wide, jnp.zeros((BLOCK, size - hi), jnp.float32)], 1)
        high = wide.astype(jnp.bfloat16)
        high_ref[lo:hi, :] = high
        low_ref[lo:hi, :] = (wide - high.astype(jnp.float32)).astype(jnp.bfloat16)


def inverse_factor(kernel, rows):
    size = kernel.shape[0]
    out = jax.ShapeDtypeStruct((size, size), jnp.bfloat16)
    return pl.pallas_call(
        factor_kernel,
        out_shape=(out, out),
        scratch_shapes=[pltpu.VMEM((size, 2 * size), jnp.float32)],
        compiler_params=pltpu.CompilerParams(vmem_limit_bytes=40 << 20),
        name="factor",
    )(kernel, rows)


def split(value):
    high = value.astype(jnp.bfloat16)
    return high, (value - high.astype(jnp.float32)).astype(jnp.bfloat16)


def product(a, b):
    return lax.dot_general(a, b, (((1,), (1,)), ((), ())), preferred_element_type=jnp.float32)


def outer_kernel(factor_ref, rows_ref, out_ref):
    high, low = split(factor_ref[...])
    rows = rows_ref[...]
    out_ref[...] = product(high, rows) + product(low, rows)


def outer(factor, rows):
    tall, depth = factor.shape
    size = rows.shape[0]
    tile = min(256, tall)
    return pl.pallas_call(
        outer_kernel,
        grid=(tall // tile,),
        in_specs=[
            pl.BlockSpec((tile, depth), lambda i: (i, 0)),
            pl.BlockSpec((size, depth), lambda i: (0, 0)),
        ],
        out_specs=pl.BlockSpec((tile, size), lambda i: (i, 0)),
        out_shape=jax.ShapeDtypeStruct((tall, size), jnp.float32),
        compiler_params=pltpu.CompilerParams(vmem_limit_bytes=40 << 20),
        name="outer",
    )(factor, rows)


def final_kernel(place_ref, a_ref, b_ref, c_ref, row_ref, col_ref, outer_ref, high_ref, low_ref, *rest):
    out_ref = rest[-1]
    tile, size = outer_ref.shape
    row, col = row_ref[...], col_ref[...]
    cosine = None
    for k, ref in enumerate((a_ref, b_ref, c_ref)):
        part = ref[...].astype(jnp.float32) * (row[:, k : k + 1] * col[k : k + 1, :])
        cosine = part if cosine is None else cosine + part
    shift = place_ref[0] + pl.program_id(0) * tile
    shape = (tile, size)
    same = lax.broadcasted_iota(jnp.int32, shape, 0) + shift == lax.broadcasted_iota(
        jnp.int32, shape, 1
    )
    cosine = jnp.where(same, row[:, 4:5], cosine)
    updated = (row[:, 3:4] * col[3:4, :]) * tangent_ratio(cosine)
    updated = jnp.where(same, updated + RIDGE, updated) - outer_ref[...]
    up, down = split(updated)
    high = high_ref[...]
    out_ref[...] = product(up, high) + (product(up, low_ref[...]) + product(down, high))


def final(place, codes, row, col, outer_part, high, low, half, previous):
    tall, size = outer_part.shape
    tile = min(128, tall // 2)
    steps = tall // 2 // tile
    whole = pl.BlockSpec((size, size), lambda i, p: (0, 0))
    here = pl.BlockSpec((tile, size), lambda i, p: (i, 0))
    there = pl.BlockSpec((tile, size), lambda i, p: (i + half * steps, 0))
    specs = [
        here,
        here,
        here,
        pl.BlockSpec((tile, 8), lambda i, p: (i, 0)),
        pl.BlockSpec((8, size), lambda i, p: (0, 0)),
        there,
        whole,
        whole,
    ]
    args = [place, *codes, row, col, outer_part, high, low]
    alias = {}
    if previous is not None:
        specs.append(pl.BlockSpec(memory_space=pl.ANY))
        args.append(previous)
        alias = {len(args) - 1: 0}
    return pl.pallas_call(
        final_kernel,
        grid_spec=pltpu.PrefetchScalarGridSpec(
            num_scalar_prefetch=1, grid=(steps,), in_specs=specs, out_specs=there
        ),
        out_shape=jax.ShapeDtypeStruct((tall, size), jnp.float32),
        input_output_aliases=alias,
        compiler_params=pltpu.CompilerParams(vmem_limit_bytes=40 << 20),
        name="final",
    )(*args)


def encode(value, bound_row, bound_col):
    scale_row = lax.rsqrt(jnp.maximum(bound_row, TINY)) * CODES
    scale_col = lax.rsqrt(jnp.maximum(bound_col, TINY))
    return jnp.round(value * scale_row[:, None] * scale_col[None, :]).astype(jnp.int16)


def body(points, factor, panel_block, finished):
    kern_rows, width = points.shape
    own_rows, depth = factor.shape
    half_rows = own_rows // 2
    fac, pair, kern = lax.axis_index("fac"), lax.axis_index("pair"), lax.axis_index("kern")
    kern_bits = bits_of("kern")
    core, ways = kern_bits[0], kern_bits[1:]
    routes = (ways, ways[::-1])
    panel_start = panel_block[0] * P_SIZE
    used_count = finished[0]

    root_kern = panel_start // kern_rows
    local_points = lax.dynamic_slice_in_dim(points, panel_start - root_kern * kern_rows, P_SIZE, 0)
    piece = halve(local_points, "kern", core, root_kern)
    parts = [piece[:, : width // 2], piece[:, width // 2 :]]
    for step in range(len(ways)):
        parts = [
            spread(part, "kern", route[step], root_kern) for part, route in zip(parts, routes)
        ]
    panel_points = join(jnp.concatenate(parts, axis=1), "kern", core)

    owner = panel_start // own_rows
    root_pair = lax.rem(owner, lax.axis_size("pair"))
    root_fac = lax.rem(owner // lax.axis_size("pair"), lax.axis_size("fac"))
    local_rows = lax.dynamic_slice_in_dim(factor, panel_start - owner * own_rows, P_SIZE, 0)
    keep = jnp.arange(depth, dtype=jnp.int32) < used_count
    local_rows = jnp.where(keep[None, :], local_rows, 0.0).astype(jnp.bfloat16)
    piece = halve(local_rows, "kern", core, root_kern)
    parts = [piece[:, : depth // 2], piece[:, depth // 2 :]]
    for step in range(len(ways)):
        parts = [
            halve(part, "kern", route[step], root_kern) for part, route in zip(parts, routes)
        ]
    piece = jnp.concatenate(parts, axis=1)
    piece = spread(piece, "pair", 0, root_pair)
    piece = spread(piece, "fac", 0, root_fac)
    parts = [piece[:, : depth // 2], piece[:, depth // 2 :]]
    for step in range(len(ways))[::-1]:
        parts = [join(part, "kern", route[step]) for part, route in zip(parts, routes)]
    panel_rows = join(jnp.concatenate(parts, axis=1), "kern", core)

    row_part = jnp.sum(jnp.square(points.astype(jnp.float32)), axis=1)
    panel_part = jnp.sum(jnp.square(panel_points.astype(jnp.float32)), axis=1)
    norms = jnp.concatenate([row_part, panel_part])
    pair_norms = exchange(norms, "pair", 0)
    both = jnp.stack([norms, pair_norms])
    far = exchange(both, "fac", 0)
    fac_norms, cross_norms = far[0], far[1]
    norm_sum = (norms + pair_norms) + (fac_norms + cross_norms)
    norm_all = norm_sum / DIN + EPS
    panel_norm = norm_all[kern_rows:]

    gather_bits = routes[0] + [core]
    order = sum(bit_of(kern, bit) << place for place, bit in enumerate(gather_bits))
    some = P_SIZE >> len(kern_bits)
    my_panel = lax.dynamic_slice_in_dim(panel_points, order * some, some, 0)
    inner = product(my_panel, panel_points)
    inner = inner + exchange(inner, "pair", 0)
    inner = inner + exchange(inner, "fac", 0)
    my_norm = lax.dynamic_slice_in_dim(panel_norm, order * some, some, 0)
    scale = jnp.sqrt(my_norm)[:, None] * jnp.sqrt(panel_norm)[None, :]
    same = (order * some + jnp.arange(some, dtype=jnp.int32))[:, None] == jnp.arange(
        P_SIZE, dtype=jnp.int32
    )[None, :]
    cosine = jnp.where(same, ((my_norm - EPS) / my_norm)[:, None], inner / DIN / scale)
    diag_kernel = scale * tangent_ratio(cosine)
    diag_kernel = jnp.where(same, diag_kernel + RIDGE, diag_kernel)
    for bit in gather_bits:
        diag_kernel = join(diag_kernel, "kern", bit)

    codes = encode(product(points, panel_points), row_part, panel_part)
    codes = codes.reshape(2, 2, 2, half_rows, P_SIZE)

    def rows_of(vector, f, p, h):
        return lax.dynamic_slice_in_dim(vector, ((f * 2 + p) * 2 + h) * half_rows, half_rows, 0)

    def cols_of(vector):
        return vector[kern_rows:]

    def block_of(value, f, p, h):
        return lax.dynamic_slice(
            value, (f, p, h, 0, 0), (1, 1, 1, half_rows, P_SIZE)
        ).reshape(half_rows, P_SIZE)

    def pick(value, index):
        return lax.dynamic_index_in_dim(value, index, 0, keepdims=False)

    def decode(code, vector, f, p, h):
        row = jnp.sqrt(rows_of(vector, f, p, h)) * (1.0 / CODES)
        return code.astype(jnp.float32) * row[:, None] * jnp.sqrt(cols_of(vector))[None, :]

    send0 = lax.dynamic_slice(
        codes, (0, 1 - pair, 0, 0, 0), (2, 1, 1, half_rows, P_SIZE)
    ).reshape(2, half_rows, P_SIZE)
    send1 = lax.dynamic_slice(
        codes, (1 - fac, 0, 1, 0, 0), (1, 2, 1, half_rows, P_SIZE)
    ).reshape(2, half_rows, P_SIZE)
    got0 = exchange(send0, "pair", 0)
    got1 = exchange(send1, "fac", 0)
    away0 = encode(
        decode(block_of(codes, 1 - fac, pair, 0), norms, 1 - fac, pair, 0)
        + decode(pick(got0, 1 - fac), pair_norms, 1 - fac, pair, 0),
        rows_of(norms + pair_norms, 1 - fac, pair, 0),
        cols_of(norms + pair_norms),
    )
    away1 = encode(
        decode(block_of(codes, fac, 1 - pair, 1), norms, fac, 1 - pair, 1)
        + decode(pick(got1, 1 - pair), fac_norms, fac, 1 - pair, 1),
        rows_of(norms + fac_norms, fac, 1 - pair, 1),
        cols_of(norms + fac_norms),
    )
    last0 = exchange(away0, "fac", 0)
    last1 = exchange(away1, "pair", 0)
    triple0 = (block_of(codes, fac, pair, 0), pick(got0, fac), last0)
    triple1 = (block_of(codes, fac, pair, 1), pick(got1, pair), last1)
    bounds0 = (norms, pair_norms, fac_norms + cross_norms)
    bounds1 = (norms, fac_norms, pair_norms + cross_norms)

    def scales(bounds, h):
        row_norm = rows_of(norm_all, fac, pair, h)
        row_scale = lax.rsqrt(row_norm) * (1.0 / (CODES * DIN))
        row = [jnp.sqrt(rows_of(b, fac, pair, h)) * row_scale for b in bounds]
        row += [jnp.sqrt(row_norm), (row_norm - EPS) / row_norm]
        row += [jnp.zeros_like(row_norm)] * 3
        col_scale = lax.rsqrt(panel_norm)
        col = [jnp.sqrt(cols_of(b)) * col_scale for b in bounds]
        col += [jnp.sqrt(panel_norm)] + [jnp.zeros_like(panel_norm)] * 4
        return jnp.stack(row, axis=1), jnp.stack(col, axis=0)

    high, low = inverse_factor(diag_kernel, panel_rows)
    outer_part = outer(factor, panel_rows)
    first_row = ((kern * 2 + fac) * 2 + pair) * own_rows - panel_start
    place0 = jnp.reshape(first_row, (1,)).astype(jnp.int32)
    row1, col1 = scales(bounds1, 1)
    out = final(place0 + half_rows, triple1, row1, col1, outer_part, high, low, 1, None)
    row0, col0 = scales(bounds0, 0)
    return final(place0, triple0, row0, col0, outer_part, high, low, 0, out)


def solution(mesh):
    placed = (P("kern", ("fac", "pair")), P(("kern", "fac", "pair"), None), P(), P())
    return jax.shard_map(
        body,
        mesh=mesh,
        in_specs=placed,
        out_specs=P(("kern", "fac", "pair"), None),
        check_vma=False,
    )
```

```python
import jax
import jax.numpy as jnp
from jax import lax
from jax.experimental import pallas as pl
from jax.experimental.pallas import tpu as pltpu
from jax.sharding import PartitionSpec as P

DIN = 3072
P_SIZE = 512
LAYERS = 5
RIDGE = 3.0
EPS = 1e-06
CODES = 32760.0
TINY = 1e-30
BLOCK = 128
ACOS = (
    1.5707963050,
    -0.2145988016,
    0.0889789874,
    -0.0501743046,
    0.0308918810,
    -0.0170881256,
    0.0066700901,
    -0.0012624911,
)


def exchange(value, axis, bit):
    size = lax.axis_size(axis)
    return lax.ppermute(value, axis, [(i, i ^ (1 << bit)) for i in range(size)])


def bit_of(index, bit):
    return lax.bitwise_and(lax.shift_right_logical(index, bit), 1)


def halve(value, axis, bit, root):
    mine = bit_of(lax.axis_index(axis), bit)
    rows = value.shape[0] // 2
    low, high = value[:rows], value[rows:]
    got = exchange(jnp.where(mine == 0, high, low), axis, bit)
    return jnp.where(mine == bit_of(root, bit), jnp.where(mine == 0, low, high), got)


def join(value, axis, bit):
    mine = bit_of(lax.axis_index(axis), bit)
    got = exchange(value, axis, bit)
    return jnp.concatenate(
        [jnp.where(mine == 0, value, got), jnp.where(mine == 0, got, value)], axis=0
    )


def spread(value, axis, bit, root):
    mine = bit_of(lax.axis_index(axis), bit)
    got = exchange(value, axis, bit)
    return jnp.where(mine == bit_of(root, bit), value, got)


def bits_of(axis):
    return list(range((lax.axis_size(axis) - 1).bit_length()))


def root_of(value):
    return value * lax.rsqrt(jnp.maximum(value, TINY))


def arc_part(cosine):
    gap = jnp.maximum(1.0 - cosine, 0.0)
    poly = jnp.full_like(cosine, ACOS[-1] / jnp.pi)
    for term in ACOS[-2::-1]:
        poly = poly * cosine + term / jnp.pi
    return root_of(gap) * poly, root_of(gap * (1.0 + cosine)) * (1.0 / jnp.pi)


def tangent_ratio(cosine):
    cosine = jnp.clip(cosine, -1.0, 1.0)
    angle, sine = arc_part(jnp.abs(cosine))
    slope = jnp.where(cosine < 0.0, angle, 1.0 - angle)
    tangent = cosine
    cosine = slope * cosine + sine
    tangent = slope * tangent + cosine
    for _ in range(LAYERS - 1):
        cosine = jnp.minimum(cosine, 1.0)
        angle, sine = arc_part(cosine)
        slope = 1.0 - angle
        cosine = slope * cosine + sine
        tangent = slope * tangent + cosine
    return tangent


def eliminate(block, unit):
    size = block.shape[0]
    groups = size // 8
    left = [block[8 * g : 8 * g + 8] for g in range(groups)]
    right = [unit[8 * g : 8 * g + 8] for g in range(groups)]
    shape = (8, size)
    sub = lax.broadcasted_iota(jnp.int32, shape, 0)
    scaled = []
    for g in range(groups):
        columns = [
            jnp.broadcast_to(left[g][:, 8 * g + k : 8 * g + k + 1], shape) for k in range(8)
        ]
        steps, left_rows, right_rows = {}, [], []
        pivots = None
        for k in range(8):
            inverse = 1.0 / jnp.broadcast_to(columns[k][k : k + 1], shape)
            pivots = inverse if pivots is None else jnp.where(sub == k, inverse, pivots)
            below = jnp.where(sub > k, columns[k], 0.0)
            left_rows.append(jnp.broadcast_to(left[g][k : k + 1], shape) * inverse)
            right_rows.append(jnp.broadcast_to(right[g][k : k + 1], shape) * inverse)
            for m in range(k + 1, 8):
                steps[k, m] = jnp.broadcast_to(columns[m][k : k + 1], shape) * inverse
                columns[m] = columns[m] - below * steps[k, m]
            if k < 7:
                left[g] = left[g] - below * left_rows[k]
                right[g] = right[g] - below * right_rows[k]
        scaled.append(right[g] * jnp.sqrt(pivots))
        for h in range(g + 1, groups):
            columns = [
                jnp.broadcast_to(left[h][:, 8 * g + k : 8 * g + k + 1], shape) for k in range(8)
            ]
            for k in range(8):
                for m in range(k + 1, 8):
                    columns[m] = columns[m] - columns[k] * steps[k, m]
                left[h] = left[h] - columns[k] * left_rows[k]
                right[h] = right[h] - columns[k] * right_rows[k]
    return jnp.concatenate(scaled, 0)


def exact_dot(a, b, dims):
    return lax.dot_general(
        a, b, (dims, ((), ())), preferred_element_type=jnp.float32, precision=lax.Precision.HIGHEST
    )


def factor_kernel(kernel_ref, rows_ref, high_ref, low_ref, work):
    size = kernel_ref.shape[0]
    blocks = size // BLOCK
    work[:, :size] = kernel_ref[...] - lax.dot_general(
        rows_ref[...],
        rows_ref[...],
        (((1,), (1,)), ((), ())),
        preferred_element_type=jnp.float32,
    )
    shape = (size, size)
    work[:, size:] = jnp.where(
        lax.broadcasted_iota(jnp.int32, shape, 0) == lax.broadcasted_iota(jnp.int32, shape, 1),
        1.0,
        0.0,
    )
    for k in range(blocks):
        lo, hi = k * BLOCK, (k + 1) * BLOCK
        small = eliminate(work[lo:hi, lo:hi], work[lo:hi, size + lo : size + hi])
        wide = small
        if k > 0:
            wide = jnp.concatenate(
                [exact_dot(small, work[lo:hi, size : size + lo], ((1,), (0,))), small], 1
            )
        if k + 1 < blocks:
            upper = exact_dot(small, work[lo:hi, hi:size], ((1,), (0,)))
            rest = exact_dot(upper, jnp.concatenate([upper, wide], 1), ((0,), (0,)))
            work[hi:size, hi : size + hi] = work[hi:size, hi : size + hi] - rest
            wide = jnp.concatenate([wide, jnp.zeros((BLOCK, size - hi), jnp.float32)], 1)
        high = wide.astype(jnp.bfloat16)
        high_ref[lo:hi, :] = high
        low_ref[lo:hi, :] = (wide - high.astype(jnp.float32)).astype(jnp.bfloat16)


def inverse_factor(kernel, rows):
    size = kernel.shape[0]
    out = jax.ShapeDtypeStruct((size, size), jnp.bfloat16)
    return pl.pallas_call(
        factor_kernel,
        out_shape=(out, out),
        scratch_shapes=[pltpu.VMEM((size, 2 * size), jnp.float32)],
        compiler_params=pltpu.CompilerParams(vmem_limit_bytes=40 << 20),
        name="factor",
    )(kernel, rows)


def split(value):
    high = value.astype(jnp.bfloat16)
    return high, (value - high.astype(jnp.float32)).astype(jnp.bfloat16)


def product(a, b):
    return lax.dot_general(a, b, (((1,), (1,)), ((), ())), preferred_element_type=jnp.float32)


def outer_kernel(factor_ref, rows_ref, out_ref):
    high, low = split(factor_ref[...])
    rows = rows_ref[...]
    out_ref[...] = product(high, rows) + product(low, rows)


def outer(factor, rows):
    tall, depth = factor.shape
    size = rows.shape[0]
    tile = min(256, tall)
    return pl.pallas_call(
        outer_kernel,
        grid=(tall // tile,),
        in_specs=[
            pl.BlockSpec((tile, depth), lambda i: (i, 0)),
            pl.BlockSpec((size, depth), lambda i: (0, 0)),
        ],
        out_specs=pl.BlockSpec((tile, size), lambda i: (i, 0)),
        out_shape=jax.ShapeDtypeStruct((tall, size), jnp.float32),
        compiler_params=pltpu.CompilerParams(vmem_limit_bytes=40 << 20),
        name="outer",
    )(factor, rows)


def codes_kernel(place_ref, points_ref, panel_ref, *refs):
    outs, col_ref = refs[:-1], refs[-1]

    @pl.when((pl.program_id(0) == 0) & (pl.program_id(1) == 0))
    def _():
        square = jnp.square(panel_ref[...].astype(jnp.float32))
        total = exact_dot(jnp.ones((8, square.shape[1]), jnp.float32), square, ((1,), (1,)))
        col_ref[...] = lax.rsqrt(jnp.maximum(total, TINY))

    rows = points_ref[...]
    wide = rows.astype(jnp.float32)
    bound = jnp.sum(wide * wide, axis=1, keepdims=True)
    scale = lax.rsqrt(jnp.maximum(bound, TINY)) * CODES
    code = jnp.round(product(rows, panel_ref[...]) * (scale * col_ref[0:1, :])).astype(jnp.int16)
    turn = pl.program_id(0)
    for k, out in enumerate(outs):

        @pl.when(turn == k)
        def _(out=out):
            out[...] = code


def codes_of(place, points, panel, first, count):
    size, width = panel.shape
    tile = points.shape[0] // 16

    def where(i, j, p):
        return ((p[0] ^ (3 - i)) * 4 + first + j, 0)

    def out_at(k):
        def index(i, j, p):
            return (jnp.clip((i - k) * count + j, 0, count - 1), 0)

        return pl.BlockSpec((tile, size), index)

    out = jax.ShapeDtypeStruct((count * tile, size), jnp.int16)
    return pl.pallas_call(
        codes_kernel,
        grid_spec=pltpu.PrefetchScalarGridSpec(
            num_scalar_prefetch=1,
            grid=(4, count),
            in_specs=[
                pl.BlockSpec((tile, width), where),
                pl.BlockSpec((size, width), lambda i, j, p: (0, 0)),
            ],
            out_specs=[out_at(k) for k in range(4)],
            scratch_shapes=[pltpu.VMEM((8, size), jnp.float32)],
        ),
        out_shape=(out,) * 4,
        compiler_params=pltpu.CompilerParams(vmem_limit_bytes=30 << 20),
        name="codes",
    )(place, points, panel)


def final_kernel(place_ref, *refs):
    codes, (row_ref, col_ref, outer_ref, high_ref, low_ref), out_ref = refs[:4], refs[4:9], refs[-1]
    tile, size = outer_ref.shape
    row, col = row_ref[...], col_ref[...]
    cosine = None
    for k, ref in enumerate(codes):
        part = ref[...].astype(jnp.float32) * (row[:, k : k + 1] * col[k : k + 1, :])
        cosine = part if cosine is None else cosine + part
    shift = place_ref[1] + pl.program_id(0) * tile
    shape = (tile, size)
    same = lax.broadcasted_iota(jnp.int32, shape, 0) + shift == lax.broadcasted_iota(
        jnp.int32, shape, 1
    )
    cosine = jnp.where(same, row[:, 5:6], cosine)
    updated = (row[:, 4:5] * col[4:5, :]) * tangent_ratio(cosine)
    updated = jnp.where(same, updated + RIDGE, updated) - outer_ref[...]
    up, down = split(updated)
    high = high_ref[...]
    out_ref[...] = product(up, high) + (product(up, low_ref[...]) + product(down, high))


def final(place, codes, row, col, outer_part, high, low, start, previous):
    tall, size = outer_part.shape
    tile = 128
    rows = codes[0].shape[0]
    whole = pl.BlockSpec((size, size), lambda i, p: (0, 0))
    here = pl.BlockSpec((tile, size), lambda i, p: (i, 0))
    there = pl.BlockSpec((tile, size), lambda i, p: (i + start // tile, 0))
    specs = [here] * 4 + [
        pl.BlockSpec((tile, 8), lambda i, p: (i, 0)),
        pl.BlockSpec((8, size), lambda i, p: (0, 0)),
        there,
        whole,
        whole,
    ]
    args = [place, *codes, row, col, outer_part, high, low]
    alias = {}
    if previous is not None:
        specs.append(pl.BlockSpec(memory_space=pl.ANY))
        args.append(previous)
        alias = {len(args) - 1: 0}
    return pl.pallas_call(
        final_kernel,
        grid_spec=pltpu.PrefetchScalarGridSpec(
            num_scalar_prefetch=1, grid=(rows // tile,), in_specs=specs, out_specs=there
        ),
        out_shape=jax.ShapeDtypeStruct((tall, size), jnp.float32),
        input_output_aliases=alias,
        compiler_params=pltpu.CompilerParams(vmem_limit_bytes=40 << 20),
        name="final",
    )(*args)


def table(vectors, axis):
    vectors = list(vectors)
    vectors += [jnp.zeros_like(vectors[0])] * (8 - len(vectors))
    return jnp.stack(vectors, axis=axis)


def panel(points, factor, panel_block, finished):
    kern_rows, _ = points.shape
    own_rows, depth = factor.shape
    fac, pair, kern = lax.axis_index("fac"), lax.axis_index("pair"), lax.axis_index("kern")
    kern_bits = bits_of("kern")
    core, ways = kern_bits[0], kern_bits[1:]
    routes = (ways, ways[::-1])
    panel_start = panel_block[0] * P_SIZE
    used_count = finished[0]
    root_kern = panel_start // kern_rows
    owner = panel_start // own_rows
    root_pair = lax.rem(owner, lax.axis_size("pair"))
    root_fac = lax.rem(owner // lax.axis_size("pair"), lax.axis_size("fac"))

    def parted(value):
        middle = value.shape[1] // 2
        return [value[:, :middle], value[:, middle:]]

    used = jnp.arange(depth, dtype=jnp.int32) < used_count
    my_core = bit_of(kern, core)
    half = P_SIZE // 2

    def points_half(side):
        start = panel_start - root_kern * kern_rows + side * half
        return lax.dynamic_slice_in_dim(points, start, half, 0)

    def rows_half(side):
        start = panel_start - owner * own_rows + side * half
        rows = lax.dynamic_slice_in_dim(factor, start, half, 0)
        return jnp.where(used[None, :], rows, 0.0).astype(jnp.bfloat16)

    got = exchange(points_half(1 - my_core), "kern", core)
    near = parted(jnp.where(my_core == bit_of(root_kern, core), points_half(my_core), got))
    got = exchange(rows_half(1 - my_core), "kern", core)
    piece = parted(jnp.where(my_core == bit_of(root_kern, core), rows_half(my_core), got))
    for step in range(len(ways)):
        for side, route in enumerate(routes):
            near[side] = spread(near[side], "kern", route[step], root_kern)
            piece[side] = halve(piece[side], "kern", route[step], root_kern)
    piece = jnp.concatenate(piece, axis=1)
    piece = spread(piece, "pair", 0, root_pair)
    panel_points = join(jnp.concatenate(near, axis=1), "kern", core)
    piece = spread(piece, "fac", 0, root_fac)

    row_part = jnp.sum(jnp.square(points.astype(jnp.float32)), axis=1)
    pair_part = exchange(row_part, "pair", 0)
    far = exchange(jnp.concatenate([row_part, pair_part]), "fac", 0)
    row_parts = [row_part, pair_part, far[:kern_rows], far[kern_rows:]]
    panel_part = jnp.sum(jnp.square(panel_points.astype(jnp.float32)), axis=1)

    gather_bits = routes[0] + [core]
    order = sum(bit_of(kern, bit) << place_bit for place_bit, bit in enumerate(gather_bits))
    some = P_SIZE >> len(kern_bits)
    my_panel = lax.dynamic_slice_in_dim(panel_points, order * some, some, 0)
    inner = product(my_panel, panel_points)
    pad = jnp.zeros((7, P_SIZE), jnp.float32)
    got = exchange(jnp.concatenate([inner, panel_part[None], pad]), "pair", 0)
    inner = inner + got[:some]
    far = exchange(
        jnp.concatenate([inner, panel_part[None], got[some : some + 1], pad[:6]]), "fac", 0
    )
    inner = inner + far[:some]
    col_parts = [panel_part, got[some], far[some], far[some + 1]]
    panel_norm = sum(col_parts) / DIN + EPS

    first_row = ((kern * 2 + fac) * 2 + pair) * own_rows
    place = jnp.stack([fac * 2 + pair, first_row - panel_start]).astype(jnp.int32)
    mine_a = codes_of(place, points, panel_points, 0, 3)
    mine_b = codes_of(place, points, panel_points, 3, 1)

    def scatter(codes):
        cross = [(i, i ^ 3) for i in range(4)]
        far_codes = lax.ppermute(codes[0], ("fac", "pair"), cross)
        fac_codes = exchange(codes[1], "fac", 0)
        pair_codes = exchange(codes[2], "pair", 0)
        return codes[3], pair_codes, fac_codes, far_codes

    codes_a = scatter(mine_a)
    codes_b = scatter(mine_b)

    my_norm = lax.dynamic_slice_in_dim(panel_norm, order * some, some, 0)
    scale = jnp.sqrt(my_norm)[:, None] * jnp.sqrt(panel_norm)[None, :]
    same = (order * some + jnp.arange(some, dtype=jnp.int32))[:, None] == jnp.arange(
        P_SIZE, dtype=jnp.int32
    )[None, :]
    cosine = jnp.where(same, ((my_norm - EPS) / my_norm)[:, None], inner / DIN / scale)
    diag_kernel = scale * tangent_ratio(cosine)
    diag_kernel = jnp.where(same, diag_kernel + RIDGE, diag_kernel)
    for bit in gather_bits:
        diag_kernel = join(diag_kernel, "kern", bit)

    piece = parted(piece)
    for step in range(len(ways))[::-1]:
        piece = [join(part, "kern", route[step]) for part, route in zip(piece, routes)]
    panel_rows = join(jnp.concatenate(piece, axis=1), "kern", core)

    mine = [
        lax.dynamic_slice_in_dim(part, (fac * 2 + pair) * own_rows, own_rows, 0)
        for part in row_parts
    ]
    row_norm = sum(mine) / DIN + EPS
    row_scale = lax.rsqrt(row_norm) * (1.0 / (CODES * DIN))
    row = [jnp.sqrt(part) * row_scale for part in mine]
    row = table(row + [jnp.sqrt(row_norm), (row_norm - EPS) / row_norm], 1)
    col_scale = lax.rsqrt(panel_norm)
    col = table([jnp.sqrt(part) * col_scale for part in col_parts] + [jnp.sqrt(panel_norm)], 0)

    outer_part = outer(factor, panel_rows)
    high, low = inverse_factor(diag_kernel, panel_rows)
    begin = own_rows * 3 // 4
    out = final(place, codes_a, row[:begin], col, outer_part, high, low, 0, None)
    place_b = place + jnp.array([0, begin], jnp.int32)
    return final(place_b, codes_b, row[begin:], col, outer_part, high, low, begin, out)


def solution(mesh):
    placed = (P("kern", ("fac", "pair")), P(("kern", "fac", "pair"), None), P(), P())
    return jax.shard_map(
        panel,
        mesh=mesh,
        in_specs=placed,
        out_specs=P(("kern", "fac", "pair"), None),
        check_vma=False,
    )
```
